32 devices in a mesh: shot: 2 (over x), tile: 16 (over z, y, core).
Axes of the slice: x: 2, y: 2, z: 4, core: 2. Of those that a mesh axis runs over, the one named last changes fastest.
Arguments:
- wave_now: float32 [4, 32, 32, 128], P('shot', 'tile'), parts along dimension 0, may hold values from -6 to 6
- wave_prev: float32 [4, 32, 32, 128], P('shot', 'tile'), parts along dimension 0, may hold values from -6 to 6
- facies: int32 [32, 32, 128], P('tile'), may hold values from 0 to 7
- velocity_table: float32 [8], replicated, may hold values from 0.05 to 0.2
- epsilon_table: float32 [8], replicated, may hold values from 0 to 0.2
- tilt_table: float32 [8], replicated, may hold values from -0.6 to 0.6
- source_cell: int32 [2], P('shot'), parts along dimension 0, may hold values from 0 to 4095
- source_wavelet: float32 [8], P('shot'), parts along dimension 0, may hold values from -8 to 8
- receiver_cells: int32 [4096], P('shot'), parts along dimension 0, may hold values from 0 to 4095
- receiver_data: float32 [4, 4096], P(None, 'shot'), parts along dimension 1, may hold values from -6 to 6
Outputs:
- filtered: bfloat16 [64, 32, 32, 128], P('shot', None, 'tile'), parts along dimension 0
- wave_out: float32 [4, 32, 32, 128], P('shot', 'tile'), parts along dimension 0
The draws below stay inside these ranges and needn't reach their ends.
There are 2 independent parts, one for each index of `shot`. The reference program is written for one: setup_inputs(seed, part) draws one part's arguments, and reference() takes and returns one part's arrays. A program takes and returns all parts, laid end to end along the dimension named above; an argument that names none is the same for every part. Nothing has to cross between parts.
Inputs may be any that keep to these rules, and one draw needn't show every extreme that they name: `source_cell`: a surface cell y * 128 + x. `receiver_cells`: surface cells y * 128 + x; cells may repeat.
All inputs are finite; a program needn't handle non-finite values.
Results may differ from the reference program's by a relative error of at most 0.001.
The reference program's roundings to bfloat16 on the way (of `snapshot` and `image`) count: a program that leaves them out, or rounds other values in their place, can miss the bound.
Values may be sent and summed in bfloat16 or wider, within the bound.
A program may use at most 64 MiB of HBM per device.

```python
import jax
import jax.numpy as jnp
from jax import lax

NX = 128
NREC = 2048
NLAG = 32
STEPS = 4
NFAC = 8
NY = 32
NZ = 32


def touch_ends(entries, key, smallest, largest):
    dims = entries.shape
    index_at = [jax.random.randint(jax.random.fold_in(key, axis), (), 0, dims[axis]) for axis in range(len(dims))]
    entries = entries.at[tuple(index_at)].set(smallest)
    longest = dims.index(max(dims))
    index_at[longest] = (index_at[longest] + 1) % dims[longest]
    return entries.at[tuple(index_at)].set(largest)


def block_scale(own_key, extent, cuts, smallest, top_value):
    factor_of, own = 1.0, jax.random.fold_in(own_key, 6)
    for dim, shards_of in cuts:
        draws = jnp.exp(jax.random.uniform(jax.random.fold_in(own, dim), (shards_of,), jnp.float32, smallest / len(cuts), top_value / len(cuts)))
        factor_of = factor_of * jnp.repeat(draws, extent[dim] // shards_of).reshape([-1 if axis == dim else 1 for axis in range(len(extent))])
    return factor_of


def centred(own_key, extent, spread, bound, shards=(), held_as=jnp.bfloat16):
    level = block_scale(own_key, extent, shards, -0.22, 0.18) if shards else 1.0
    values = jax.random.normal(own_key, extent, jnp.float32) * spread * level
    return jnp.minimum(jnp.maximum(values, -bound), bound).astype(held_as)


def setup_inputs(seed: int = 0, part: int = 0) -> dict:
    splits = jax.random.split(jax.random.key(seed), 11)
    own_keys = jax.random.split(jax.random.fold_in(splits[10], part), 11)
    return {
        "wave_now": centred(own_keys[0], (2, NY, NZ, NX), 1.0, 6.0, ((1, 16),), jnp.float32),
        "wave_prev": centred(own_keys[1], (2, NY, NZ, NX), 1.0, 6.0, ((1, 16),), jnp.float32),
        "facies": touch_ends(jax.random.randint(splits[2], (NY, NZ, NX), 0, NFAC), jax.random.fold_in(splits[2], 1), 0, NFAC - 1).astype(jnp.int32),
        "velocity_table": jnp.clip(jax.random.uniform(splits[3], (NFAC,), jnp.float32, 0.05, 0.2), 0.05, 0.2),
        "epsilon_table": jnp.clip(jax.random.uniform(splits[4], (NFAC,), jnp.float32, 0.0, 0.2), 0.0, 0.2),
        "tilt_table": jnp.clip(jax.random.uniform(splits[5], (NFAC,), jnp.float32, -0.6, 0.6), -0.6, 0.6),
        "source_cell": jax.random.randint(own_keys[6], (1,), 0, NY * NX).astype(jnp.int32),
        "source_wavelet": centred(own_keys[7], (STEPS,), 2.0, 8.0, (), jnp.float32),
        "receiver_cells": touch_ends(jax.random.randint(own_keys[8], (NREC,), 0, NY * NX), jax.random.fold_in(own_keys[8], 1), 0, (NY * NX) - 1).astype(jnp.int32),
        "receiver_data": centred(own_keys[9], (STEPS, NREC), 1.0, 6.0, (), jnp.float32),
    }


def wave_update(padded, previous, velocity, aniso, tilt):
    center = padded[:, 1:-1, 1:-1, 1:-1]
    along_x = padded[:, 1:-1, 1:-1, 2:] + padded[:, 1:-1, 1:-1, :-2] - 2.0 * center
    along_y = padded[:, 2:, 1:-1, 1:-1] + padded[:, :-2, 1:-1, 1:-1] - 2.0 * center
    along_z = padded[:, 1:-1, 2:, 1:-1] + padded[:, 1:-1, :-2, 1:-1] - 2.0 * center
    mixed = padded[:, 1:-1, 2:, 2:] - padded[:, 1:-1, :-2, 2:] - padded[:, 1:-1, 2:, :-2] + padded[:, 1:-1, :-2, :-2]
    operator = aniso * (along_x + along_y) + along_z + 0.25 * tilt * mixed
    return 2.0 * center - previous + velocity * operator


def filter_planes(extended):
    values = extended.astype(jnp.float32)
    spec = [(0, 0)] * (values.ndim - 3) + [(1, 1), (0, 0), (1, 1)]
    padded = jnp.pad(values, spec)
    center = padded[..., 1:-1, 1:-1, 1:-1]
    neighbours = padded[..., 2:, 1:-1, 1:-1] + padded[..., :-2, 1:-1, 1:-1]
    neighbours = neighbours + padded[..., 1:-1, 2:, 1:-1] + padded[..., 1:-1, :-2, 1:-1]
    neighbours = neighbours + padded[..., 1:-1, 1:-1, 2:] + padded[..., 1:-1, 1:-1, :-2]
    return (0.125 * (6.0 * center - neighbours)).astype(jnp.bfloat16)


def reference(wave_now, wave_prev, facies, velocity_table, epsilon_table, tilt_table, source_cell, source_wavelet, receiver_cells, receiver_data):
    velocity = velocity_table[facies]
    aniso = 1.0 + 2.0 * epsilon_table[facies]
    tilt = tilt_table[facies]
    current, previous = wave_now, wave_prev
    snapshots = []
    for step in range(STEPS):
        padded = jnp.pad(current, ((0, 0), (1, 1), (1, 1), (1, 1)))
        advanced = wave_update(padded, previous, velocity, aniso, tilt)
        source_plane = jnp.zeros((NY * NX,), jnp.float32).at[source_cell].add(jnp.broadcast_to(source_wavelet[step], source_cell.shape))
        receiver_plane = jnp.zeros((NY * NX,), jnp.float32).at[receiver_cells].add(receiver_data[step])
        surface = jnp.stack([source_plane, receiver_plane]).reshape(2, NY, NX)
        advanced = advanced.at[:, :, 0, :].add(surface)
        previous, current = current, advanced
        if step % 2 == 1:
            snapshots.append(current.astype(jnp.bfloat16))
    margin = NLAG // 2
    padded_pairs = []
    for snapshot in snapshots:
        source_padded = jnp.pad(snapshot[0].astype(jnp.float32), ((0, 0), (0, 0), (margin, margin)))
        receiver_padded = jnp.pad(snapshot[1].astype(jnp.float32), ((0, 0), (0, 0), (margin, margin)))
        padded_pairs.append((source_padded, receiver_padded))

    def one_offset(index):
        offset = index - margin
        summed = jnp.zeros((NY, NZ, NX), jnp.float32)
        for source_padded, receiver_padded in padded_pairs:
            left_part = lax.dynamic_slice_in_dim(source_padded, (margin - offset).astype(jnp.int32), NX, 2)
            right_part = lax.dynamic_slice_in_dim(receiver_padded, (margin + offset).astype(jnp.int32), NX, 2)
            summed = summed + left_part * right_part
        image = summed.astype(jnp.bfloat16)
        extended = jnp.pad(image, ((0, 0), (1, 1), (0, 0)))
        return filter_planes(extended[None])[0]

    filtered = lax.map(one_offset, jnp.arange(NLAG, dtype=jnp.int32))
    return filtered, current
```

```python
import functools

import jax
import jax.numpy as jnp
from jax import lax
from jax.experimental import pallas as pl
from jax.experimental.pallas import tpu as pltpu
from jax.sharding import PartitionSpec as P

NLAG = 32
STEPS = 4
HALO = 2
PARTS = 4


def in_order(count, body):
    def run(i, carry):
        body(i)
        return carry

    lax.fori_loop(0, count, run, 0)


def kernel(
    tiles,
    now,
    prev,
    facies,
    vel_tab,
    eps_tab,
    tilt_tab,
    src_cell,
    wavelet,
    cells,
    data,
    out,
    wave_out,
    ext0,
    ext1,
    mid0,
    mid1,
    prev_halo,
    fac_halo,
    coef,
    lhs,
    surf,
    turned,
    send,
    recv,
    planes,
    part_image,
    staged,
    halo_send,
    halo_recv,
    snap_send,
    snap_recv,
):
    rows, depth, cols = facies.shape
    per = depth // tiles
    nrec = data.shape[1]
    ext_rows = rows + 2
    group = 2 * rows
    block = (per + 2) * group
    margin = NLAG // 2
    me = lax.axis_index("tile")
    has_up = me > 0
    has_down = me < tiles - 1

    barrier = pltpu.get_barrier_semaphore()

    def greet(i):
        peer = lax.rem(me + 1 + i, tiles)
        pl.semaphore_signal(barrier, inc=1, device_id={"tile": peer})

    in_order(tiles - 1, greet)

    cell = cells[...]
    column = cell & (cols - 1) if cols & (cols - 1) == 0 else lax.rem(cell, cols)
    onehot = (lax.broadcasted_iota(jnp.int32, (cols, nrec), 0) == column).astype(jnp.float32)
    onehot = onehot.astype(jnp.bfloat16)
    amounts = data[...]
    high = amounts.astype(jnp.bfloat16).astype(jnp.float32)
    rest = amounts - high
    middle = rest.astype(jnp.bfloat16).astype(jnp.float32)
    parts = (high, middle, rest - middle, jnp.zeros_like(high))
    for i in range(ext_rows):
        first = (me * rows + i - 1) * cols
        inside = (cell >= first) & (cell < first + cols)
        for p, part in enumerate(parts):
            at = (i * PARTS + p) * STEPS
            lhs[at : at + STEPS, :] = jnp.where(inside, part, 0.0)
    surf[...] = lax.dot_general(
        lhs[...].astype(jnp.bfloat16), onehot, (((1,), (1,)), ((), ())),
        preferred_element_type=jnp.float32,
    )

    def fill_coef(i, kinds):
        vel = jnp.zeros((depth, cols), jnp.float32)
        eps, tlt = vel, vel
        for n in range(vel_tab.shape[0]):
            here = kinds == n
            vel = jnp.where(here, vel_tab[n], vel)
            eps = jnp.where(here, eps_tab[n], eps)
            tlt = jnp.where(here, tilt_tab[n], tlt)
        coef[0, i] = vel
        coef[1, i] = 1.0 + 2.0 * eps
        coef[2, i] = 0.25 * tlt

    for i in range(rows):
        fill_coef(i + 1, facies[i])
    for f in range(2):
        for i in range(rows):
            ext0[f, i + HALO] = now[f, i]
    zero_plane = jnp.zeros((depth, cols), jnp.float32)
    turned[0:group, :] = jnp.zeros((group, cols), jnp.float32)
    turned[group * (depth + 1) : group * (depth + 2), :] = jnp.zeros((group, cols), jnp.float32)

    def clear_side(side, row):
        for f in range(2):
            for i in range(HALO):
                ext0[f, row + i] = zero_plane
                ext1[f, row + i] = zero_plane
            prev_halo[side, f] = zero_plane
        fac_halo[side] = jnp.full((depth, cols), -1, jnp.int32)

    @pl.when(jnp.logical_not(has_up))
    def _():
        clear_side(0, 0)

    @pl.when(jnp.logical_not(has_down))
    def _():
        clear_side(1, rows + HALO)

    pl.semaphore_wait(barrier, tiles - 1)

    def remote(src, dst, ssem, rsem, peer):
        return pltpu.make_async_remote_copy(
            src_ref=src, dst_ref=dst, send_sem=ssem, recv_sem=rsem, device_id={"tile": peer}
        )

    def halo_copies(side):
        peer = me - 1 if side == 0 else me + 1
        first = 0 if side == 0 else rows - HALO
        edge = 0 if side == 0 else rows - 1
        other = 1 - side
        into = rows + HALO if side == 0 else 0
        sems = lambda n: (halo_send.at[side, n], halo_recv.at[other, n], peer)
        return (
            remote(now.at[:, first : first + HALO], ext0.at[:, into : into + HALO], *sems(0)),
            remote(facies.at[edge], fac_halo.at[other], *sems(1)),
            remote(prev.at[:, edge], prev_halo.at[other], *sems(2)),
        )

    def wave_copy(side):
        peer = me - 1 if side == 0 else me + 1
        first = HALO if side == 0 else rows
        into = rows + HALO if side == 0 else 0
        return remote(
            ext1.at[:, first : first + HALO], ext1.at[:, into : into + HALO],
            halo_send.at[side, 3], halo_recv.at[1 - side, 3], peer,
        )

    def arrivals(side, count):
        into = 0 if side == 0 else rows + HALO
        peer = me
        sems = lambda n: (halo_send.at[side, n], halo_recv.at[side, n], peer)
        if count == 3:
            return (
                remote(now.at[:, 0:HALO], ext0.at[:, into : into + HALO], *sems(0)),
                remote(facies.at[0], fac_halo.at[side], *sems(1)),
                remote(prev.at[:, 0], prev_halo.at[side], *sems(2)),
            )
        return (remote(ext1.at[:, HALO : 2 * HALO], ext1.at[:, into : into + HALO], *sems(3)),)

    def each_side(action):
        for side, there in ((0, has_up), (1, has_down)):
            @pl.when(there)
            def _():
                action(side)

    def start_halo(side):
        for copy in halo_copies(side):
            copy.start()

    def wait_halo(side):
        for copy in arrivals(side, 3):
            copy.wait_recv()

    def wait_wave(side):
        for copy in arrivals(side, 1):
            copy.wait_recv()

    each_side(start_halo)
    each_side(wait_halo)
    fill_coef(0, fac_halo[0])
    fill_coef(rows + 1, fac_halo[1])

    lane = lax.broadcasted_iota(jnp.int32, (depth, cols), 1)
    level = lax.broadcasted_iota(jnp.int32, (depth, cols), 0)
    first_lane, last_lane = lane == 0, lane == cols - 1
    first_level, last_level = level == 0, level == depth - 1
    surface_lane = lax.broadcasted_iota(jnp.int32, (1, cols), 1)

    def advance(step, f, i, current, above, below, old):
        right = lambda v: jnp.where(last_lane, 0.0, pltpu.roll(v, cols - 1, 1))
        left = lambda v: jnp.where(first_lane, 0.0, pltpu.roll(v, 1, 1))
        deeper = jnp.where(last_level, 0.0, pltpu.roll(current, depth - 1, 0))
        higher = jnp.where(first_level, 0.0, pltpu.roll(current, 1, 0))
        twice = 2.0 * current
        along_x = right(current) + left(current) - twice
        along_y = above + below - twice
        along_z = deeper + higher - twice
        slope = deeper - higher
        mixed = right(slope) - left(slope)
        operator = coef[1, i] * (along_x + along_y) + along_z + coef[2, i] * mixed
        new = twice - old + coef[0, i] * operator
        if f == 0:
            target = src_cell[0] - (me * rows + i - 1) * cols
            added = jnp.where(surface_lane == target, wavelet[step], 0.0)
        else:
            at = i * PARTS * STEPS + step
            added = surf[at : at + 1, :]
            for p in range(1, 3):
                added = added + surf[at + p * STEPS : at + p * STEPS + 1, :]
        return new + jnp.where(first_level, added, 0.0)

    def outer_step(step, ext, before, into):
        for f in range(2):
            for i in range(ext_rows):
                into[f, i] = advance(
                    step, f, i, ext[f, i + 1], ext[f, i], ext[f, i + 2], before(f, i)
                )

    def inner_step(step, mid, before, store):
        for f in range(2):
            for i in range(rows):
                new = advance(
                    step, f, i + 1, mid[f, i + 1], mid[f, i], mid[f, i + 2], before[f, i + HALO]
                )
                store(f, i, new)
                turned[pl.ds(group + f * rows + i, depth, stride=group), :] = new

    def prev_row(f, i):
        if i == 0:
            return prev_halo[0, f]
        if i == rows + 1:
            return prev_halo[1, f]
        return prev[f, i - 1]

    def pack_snapshot(s):
        for d in range(tiles):
            at = d * per * group
            send[s, d] = turned[at : at + block, :].astype(jnp.bfloat16)

    def snap_copy(s, peer):
        return remote(
            send.at[s, peer], recv.at[s, me], snap_send.at[s, peer], snap_recv.at[s, me], peer
        )

    def send_snapshot(s):
        in_order(tiles - 1, lambda i: snap_copy(s, lax.rem(me + 1 + i, tiles)).start())
        recv[s, me] = send[s, me]

    def await_snapshot(s):
        def body(i):
            peer = lax.rem(me + 1 + i, tiles)
            remote(
                send.at[s, me], recv.at[s, peer], snap_send.at[s, me], snap_recv.at[s, peer], peer
            ).wait_recv()

        in_order(tiles - 1, body)

    def open_snapshot(s):
        staged[...] = recv[s].reshape(tiles * block, cols).astype(jnp.float32)
        for f in range(2):
            for j in range(per + 2):
                for r in range(rows):
                    at = (j * rows + r) * tiles
                    planes[s, f, at : at + tiles, :] = staged[
                        pl.ds(j * group + f * rows + r, tiles, stride=block), :
                    ]

    outer_step(0, ext0, prev_row, mid0)

    def keep_ext1(f, i, new):
        ext1[f, i + HALO] = new

    inner_step(1, mid0, ext0, keep_ext1)
    each_side(lambda side: wave_copy(side).start())
    pack_snapshot(0)
    send_snapshot(0)
    each_side(wait_wave)
    outer_step(2, ext1, lambda f, i: mid0[f, i], mid1)

    def keep_out(f, i, new):
        wave_out[f, i] = new

    inner_step(3, mid1, ext1, keep_out)
    pack_snapshot(1)
    send_snapshot(1)

    await_snapshot(0)
    open_snapshot(0)

    def pulled(s, k):
        shift = lax.rem(2 * margin - 2 * k + 2 * cols, cols)
        return planes[s, 0] * pltpu.roll(planes[s, 1], shift, 1)

    def first_products(k):
        part_image[k] = pulled(0, k)

    in_order(NLAG, first_products)
    await_snapshot(1)
    open_snapshot(1)

    image_rows = (per + 2) * rows * tiles
    plane_rows = rows * tiles
    image_lane = lax.broadcasted_iota(jnp.int32, (1, cols), 1)
    tile_index = lax.broadcasted_iota(jnp.int32, (tiles, cols), 0)

    def finish(k):
        h = k - margin
        far = image_lane + 2 * h
        valid = (far >= 0) & (far < cols)
        image = jnp.where(valid, part_image[k] + pulled(1, k), 0.0)
        image = image.astype(jnp.bfloat16).astype(jnp.float32)
        own = image[plane_rows : plane_rows * (per + 1)]
        at_first = image_lane == lax.rem(cols - h, cols)
        at_last = image_lane == lax.rem(2 * cols - 1 - h, cols)
        total = jnp.where(at_first, 0.0, pltpu.roll(own, 1, 1))
        total = total + jnp.where(at_last, 0.0, pltpu.roll(own, cols - 1, 1))
        total = total + image[: plane_rows * per] + image[2 * plane_rows :]
        pieces = []
        for z in range(per):
            for r in range(rows):
                here = lambda q: own[z * plane_rows + q * tiles : z * plane_rows + (q + 1) * tiles]
                if r > 0:
                    low = here(r - 1)
                else:
                    low = jnp.where(tile_index == 0, 0.0, pltpu.roll(here(rows - 1), 1, 0))
                if r < rows - 1:
                    high = here(r + 1)
                else:
                    high = jnp.where(
                        tile_index == tiles - 1, 0.0, pltpu.roll(here(0), tiles - 1, 0)
                    )
                pieces.append(low + high)
        total = total + jnp.concatenate(pieces, axis=0)
        result = 0.125 * (6.0 * own - total)
        result = pltpu.roll(result, lax.rem(h + cols, cols), 1)
        for z in range(per):
            for r in range(rows):
                at = z * plane_rows + r * tiles
                staged[pl.ds(r * per + z, tiles, stride=rows * per), :] = result[at : at + tiles]
        out[k] = staged[0 : plane_rows * per, :].astype(jnp.bfloat16)

    in_order(NLAG, finish)

    def sent(side):
        for copy in halo_copies(side):
            copy.wait_send()
        wave_copy(side).wait_send()

    each_side(sent)
    for s in range(2):
        in_order(tiles - 1, lambda i: snap_copy(s, lax.rem(me + 1 + i, tiles)).wait_send())


def shards(tiles, now, prev, facies, vel, eps, tilt, src_cell, wavelet, cells, data):
    rows, depth, cols = facies.shape
    per = depth // tiles
    nrec = cells.shape[0]
    block = (per + 2) * 2 * rows
    image_rows = (per + 2) * rows * tiles
    f32 = jnp.float32
    vmem = pl.BlockSpec(memory_space=pltpu.VMEM)
    smem = pl.BlockSpec(memory_space=pltpu.SMEM)
    lhs_rows = (rows + 2) * PARTS * STEPS
    filtered, wave = pl.pallas_call(
        functools.partial(kernel, tiles),
        out_shape=(
            jax.ShapeDtypeStruct((NLAG, rows * tiles * per, cols), jnp.bfloat16),
            jax.ShapeDtypeStruct(now.shape, f32),
        ),
        in_specs=[vmem] * 3 + [smem] * 5 + [vmem] * 2,
        out_specs=(vmem, vmem),
        scratch_shapes=[
            pltpu.VMEM((2, rows + 2 * HALO, depth, cols), f32),
            pltpu.VMEM((2, rows + 2 * HALO, depth, cols), f32),
            pltpu.VMEM((2, rows + 2, depth, cols), f32),
            pltpu.VMEM((2, rows + 2, depth, cols), f32),
            pltpu.VMEM((2, 2, depth, cols), f32),
            pltpu.VMEM((2, depth, cols), jnp.int32),
            pltpu.VMEM((3, rows + 2, depth, cols), f32),
            pltpu.VMEM((lhs_rows, nrec), f32),
            pltpu.VMEM((lhs_rows, cols), f32),
            pltpu.VMEM((2 * rows * (depth + 2), cols), f32),
            pltpu.VMEM((2, tiles, block, cols), jnp.bfloat16),
            pltpu.VMEM((2, tiles, block, cols), jnp.bfloat16),
            pltpu.VMEM((2, 2, image_rows, cols), f32),
            pltpu.VMEM((NLAG, image_rows, cols), f32),
            pltpu.VMEM((tiles * block, cols), f32),
            pltpu.SemaphoreType.DMA((2, 4)),
            pltpu.SemaphoreType.DMA((2, 4)),
            pltpu.SemaphoreType.DMA((2, tiles)),
            pltpu.SemaphoreType.DMA((2, tiles)),
        ],
        compiler_params=pltpu.CompilerParams(collective_id=0, has_side_effects=True),
    )(now, prev, facies, vel, eps, tilt, src_cell, wavelet, cells.reshape(1, nrec), data)
    return filtered.reshape(NLAG, rows * tiles, per, cols), wave


def solution(mesh):
    return jax.shard_map(
        functools.partial(shards, mesh.shape["tile"]),
        mesh=mesh,
        in_specs=(
            P("shot", "tile", None, None),
            P("shot", "tile", None, None),
            P("tile", None, None),
            P(),
            P(),
            P(),
            P("shot"),
            P("shot"),
            P("shot"),
            P(None, "shot"),
        ),
        out_specs=(P("shot", None, "tile", None), P("shot", "tile", None, None)),
        check_vma=False,
    )
```

```python
import functools

import jax
import jax.numpy as jnp
from jax import lax
from jax.experimental import pallas as pl
from jax.experimental.pallas import tpu as pltpu
from jax.sharding import PartitionSpec as P

NLAG = 32
STEPS = 4
HALO = 2
UNROLL = 4
REACH = 4
PARTS = 4


def in_order(count, body):
    def run(i, carry):
        body(i)
        return carry

    lax.fori_loop(0, count, run, 0)


def kernel(
    tiles,
    now,
    prev_in,
    facies_in,
    vel_in,
    eps_in,
    tilt_in,
    src_in,
    wavelet_in,
    cells_in,
    data_in,
    out_hbm,
    wave_hbm,
    prev,
    facies,
    vel_tab,
    eps_tab,
    tilt_tab,
    src_cell,
    wavelet,
    cells,
    data,
    out,
    wave_out,
    ext0,
    ext1,
    mid0,
    mid1,
    prev_halo,
    fac_halo,
    coef,
    lhs,
    surf,
    turned,
    send,
    recv,
    planes,
    part_image,
    staged,
    woven,
    halo_send,
    halo_recv,
    snap_send,
    snap_recv,
    load_sem,
    store_sem,
    near_sem,
):
    rows, depth, cols = facies.shape
    per = depth // tiles
    nrec = data.shape[1]
    ext_rows = rows + 2
    group = 2 * rows
    block = (per + 2) * group
    margin = NLAG // 2
    me = lax.axis_index("tile")
    has_up = me > 0
    has_down = me < tiles - 1

    barrier = pltpu.get_barrier_semaphore()

    def signal_at(semaphore, step):
        for way in (-step, step):
            peer = me + way
            there = (peer >= 0) & (peer < tiles)

            @pl.when(there)
            def _():
                pl.semaphore_signal(semaphore, inc=1, device_id={"tile": peer})

    def wait_at(semaphore, step):
        lower = (me >= step).astype(jnp.int32)
        pl.semaphore_wait(semaphore, lower + (me + step < tiles).astype(jnp.int32))

    near = range(1, min(REACH, tiles - 1) + 1)
    for step in near:
        signal_at(barrier, step)

    reaches = []
    while (REACH << len(reaches)) < tiles - 1:
        reaches.append(REACH << len(reaches))

    loads = [
        pltpu.make_async_copy(src, dst, load_sem.at[n])
        for n, (src, dst) in enumerate(
            (
                (cells_in, cells),
                (data_in, data),
                (facies_in, facies),
                (vel_in, vel_tab),
                (eps_in, eps_tab),
                (tilt_in, tilt_tab),
                (src_in, src_cell),
                (wavelet_in, wavelet),
                (now, ext0.at[:, HALO : HALO + rows]),
                (prev_in, prev),
            )
        )
    ]
    for load in loads:
        load.start()
    zero_plane = jnp.zeros((depth, cols), jnp.float32)
    def clear_side(side, row):
        for f in range(2):
            for i in range(HALO):
                ext0[f, row + i] = zero_plane
                ext1[f, row + i] = zero_plane
            prev_halo[side, f] = zero_plane
        fac_halo[side] = jnp.full((depth, cols), -1, jnp.int32)

    @pl.when(jnp.logical_not(has_up))
    def _():
        clear_side(0, 0)

    @pl.when(jnp.logical_not(has_down))
    def _():
        clear_side(1, rows + HALO)

    reach = min(REACH, tiles - 1)
    pl.semaphore_wait(barrier, jnp.minimum(me, reach) + jnp.minimum(tiles - 1 - me, reach))

    def remote(src, dst, ssem, rsem, peer):
        return pltpu.make_async_remote_copy(
            src_ref=src, dst_ref=dst, send_sem=ssem, recv_sem=rsem, device_id={"tile": peer}
        )

    def halo_copies(side):
        peer = me - 1 if side == 0 else me + 1
        first = 0 if side == 0 else rows - HALO
        edge = 0 if side == 0 else rows - 1
        other = 1 - side
        into = rows + HALO if side == 0 else 0
        sems = lambda n: (halo_send.at[side, n], halo_recv.at[other, n], peer)
        return (
            remote(now.at[:, first : first + HALO], ext0.at[:, into : into + HALO], *sems(0)),
            remote(facies_in.at[edge], fac_halo.at[other], *sems(1)),
            remote(prev_in.at[:, edge], prev_halo.at[other], *sems(2)),
        )

    def wave_copy(side):
        peer = me - 1 if side == 0 else me + 1
        first = HALO if side == 0 else rows
        into = rows + HALO if side == 0 else 0
        return remote(
            ext1.at[:, first : first + HALO], ext1.at[:, into : into + HALO],
            halo_send.at[side, 3], halo_recv.at[1 - side, 3], peer,
        )

    def arrivals(side, count):
        into = 0 if side == 0 else rows + HALO
        peer = me
        sems = lambda n: (halo_send.at[side, n], halo_recv.at[side, n], peer)
        if count == 3:
            return (
                remote(now.at[:, 0:HALO], ext0.at[:, into : into + HALO], *sems(0)),
                remote(facies_in.at[0], fac_halo.at[side], *sems(1)),
                remote(prev_in.at[:, 0], prev_halo.at[side], *sems(2)),
            )
        return (remote(ext1.at[:, HALO : 2 * HALO], ext1.at[:, into : into + HALO], *sems(3)),)

    def each_side(action):
        for side, there in ((0, has_up), (1, has_down)):
            @pl.when(there)
            def _():
                action(side)

    def start_halo(side):
        for copy in halo_copies(side):
            copy.start()

    def wait_halo(side):
        for copy in arrivals(side, 3):
            copy.wait_recv()

    def wait_wave(side):
        for copy in arrivals(side, 1):
            copy.wait_recv()

    each_side(start_halo)
    if reaches:
        signal_at(near_sem.at[0], reaches[0])

    for load in loads[:2]:
        load.wait()

    cell = cells[...]
    column = cell & (cols - 1) if cols & (cols - 1) == 0 else lax.rem(cell, cols)
    onehot = (lax.broadcasted_iota(jnp.int32, (cols, nrec), 0) == column).astype(jnp.float32)
    onehot = onehot.astype(jnp.bfloat16)
    amounts = data[...]
    high = amounts.astype(jnp.bfloat16).astype(jnp.float32)
    rest = amounts - high
    middle = rest.astype(jnp.bfloat16).astype(jnp.float32)
    parts = (high, middle, rest - middle, jnp.zeros_like(high))
    for i in range(ext_rows):
        first = (me * rows + i - 1) * cols
        inside = (cell >= first) & (cell < first + cols)
        for p, part in enumerate(parts):
            at = (i * PARTS + p) * STEPS
            lhs[at : at + STEPS, :] = jnp.where(inside, part, 0.0)
    surf[...] = lax.dot_general(
        lhs[...].astype(jnp.bfloat16), onehot, (((1,), (1,)), ((), ())),
        preferred_element_type=jnp.float32,
    )

    def fill_coef(i, kinds):
        vel = jnp.zeros((depth, cols), jnp.float32)
        eps, tlt = vel, vel
        for n in range(vel_tab.shape[0]):
            here = kinds == n
            vel = jnp.where(here, vel_tab[n], vel)
            eps = jnp.where(here, eps_tab[n], eps)
            tlt = jnp.where(here, tilt_tab[n], tlt)
        coef[0, i] = vel
        coef[1, i] = 1.0 + 2.0 * eps
        coef[2, i] = 0.25 * tlt

    for load in loads[2:]:
        load.wait()
    for i in range(rows):
        fill_coef(i + 1, facies[i])
    turned[0:group, :] = jnp.zeros((group, cols), jnp.float32)
    turned[group * (depth + 1) : group * (depth + 2), :] = jnp.zeros((group, cols), jnp.float32)

    each_side(wait_halo)
    if reaches:
        wait_at(near_sem.at[0], reaches[0])
    if len(reaches) > 1:
        signal_at(near_sem.at[1], reaches[1])
    fill_coef(0, fac_halo[0])
    fill_coef(rows + 1, fac_halo[1])

    lane = lax.broadcasted_iota(jnp.int32, (depth, cols), 1)
    level = lax.broadcasted_iota(jnp.int32, (depth, cols), 0)
    first_lane, last_lane = lane == 0, lane == cols - 1
    first_level, last_level = level == 0, level == depth - 1
    surface_lane = lax.broadcasted_iota(jnp.int32, (1, cols), 1)

    def advance(step, f, i, current, above, below, old):
        right = lambda v: jnp.where(last_lane, 0.0, pltpu.roll(v, cols - 1, 1))
        left = lambda v: jnp.where(first_lane, 0.0, pltpu.roll(v, 1, 1))
        deeper = jnp.where(last_level, 0.0, pltpu.roll(current, depth - 1, 0))
        higher = jnp.where(first_level, 0.0, pltpu.roll(current, 1, 0))
        twice = 2.0 * current
        along_x = right(current) + left(current) - twice
        along_y = above + below - twice
        along_z = deeper + higher - twice
        slope = deeper - higher
        mixed = right(slope) - left(slope)
        operator = coef[1, i] * (along_x + along_y) + along_z + coef[2, i] * mixed
        new = twice - old + coef[0, i] * operator
        if f == 0:
            target = src_cell[0] - (me * rows + i - 1) * cols
            added = jnp.where(surface_lane == target, wavelet[step], 0.0)
        else:
            at = i * PARTS * STEPS + step
            added = surf[at : at + 1, :]
            for p in range(1, 3):
                added = added + surf[at + p * STEPS : at + p * STEPS + 1, :]
        return new + jnp.where(first_level, added, 0.0)

    def outer_step(step, ext, before, into):
        for f in range(2):
            for i in range(ext_rows):
                into[f, i] = advance(
                    step, f, i, ext[f, i + 1], ext[f, i], ext[f, i + 2], before(f, i)
                )

    def inner_step(step, mid, before, store):
        for f in range(2):
            for i in range(rows):
                new = advance(
                    step, f, i + 1, mid[f, i + 1], mid[f, i], mid[f, i + 2], before[f, i + HALO]
                )
                store(f, i, new)
                turned[pl.ds(group + f * rows + i, depth, stride=group), :] = new

    def prev_row(f, i):
        if i == 0:
            return prev_halo[0, f]
        if i == rows + 1:
            return prev_halo[1, f]
        return prev[f, i - 1]

    def pack_snapshot(s):
        for d in range(tiles):
            at = d * per * group
            send[s, d] = turned[at : at + block, :].astype(jnp.bfloat16)

    def snap_copy(s, peer):
        return remote(
            send.at[s, peer], recv.at[s, me], snap_send.at[s, peer], snap_recv.at[s, me], peer
        )

    def send_snapshot(s):
        in_order(tiles - 1, lambda i: snap_copy(s, lax.rem(me + 1 + i, tiles)).start())
        recv[s, me] = send[s, me]

    def await_snapshot(s):
        def body(i):
            peer = lax.rem(me + 1 + i, tiles)
            remote(
                send.at[s, me], recv.at[s, peer], snap_send.at[s, me], snap_recv.at[s, peer], peer
            ).wait_recv()

        in_order(tiles - 1, body)

    def open_snapshot(s):
        staged[...] = recv[s].reshape(tiles * block, cols).astype(jnp.float32)
        for f in range(2):
            for j in range(per + 2):
                for r in range(rows):
                    at = (j * rows + r) * tiles
                    planes[s, f, at : at + tiles, :] = staged[
                        pl.ds(j * group + f * rows + r, tiles, stride=block), :
                    ]

    outer_step(0, ext0, prev_row, mid0)

    def keep_ext1(f, i, new):
        ext1[f, i + HALO] = new

    inner_step(1, mid0, ext0, keep_ext1)
    each_side(lambda side: wave_copy(side).start())
    pack_snapshot(0)
    each_side(wait_wave)
    for n in range(1, len(reaches)):
        wait_at(near_sem.at[n], reaches[n])
        if n + 1 < len(reaches):
            signal_at(near_sem.at[n + 1], reaches[n + 1])
    send_snapshot(0)
    outer_step(2, ext1, lambda f, i: mid0[f, i], mid1)

    def keep_out(f, i, new):
        wave_out[f, i] = new

    inner_step(3, mid1, ext1, keep_out)
    pack_snapshot(1)
    send_snapshot(1)
    wave_store = pltpu.make_async_copy(wave_out, wave_hbm, store_sem.at[NLAG // UNROLL])
    wave_store.start()

    await_snapshot(0)
    open_snapshot(0)

    def pulled(s, k):
        shift = lax.rem(2 * margin - 2 * k + 2 * cols, cols)
        return planes[s, 0] * pltpu.roll(planes[s, 1], shift, 1)

    def first_products(k):
        part_image[k] = pulled(0, k)

    in_order(NLAG, first_products)
    await_snapshot(1)
    open_snapshot(1)

    image_rows = (per + 2) * rows * tiles
    plane_rows = rows * tiles
    image_lane = lax.broadcasted_iota(jnp.int32, (1, cols), 1)
    tile_index = lax.broadcasted_iota(jnp.int32, (tiles, cols), 0)

    def finish(u, k):
        h = k - margin
        far = image_lane + 2 * h
        valid = (far >= 0) & (far < cols)
        image = jnp.where(valid, part_image[k] + pulled(1, k), 0.0)
        image = image.astype(jnp.bfloat16).astype(jnp.float32)
        own = image[plane_rows : plane_rows * (per + 1)]
        at_first = image_lane == lax.rem(cols - h, cols)
        at_last = image_lane == lax.rem(2 * cols - 1 - h, cols)
        total = jnp.where(at_first, 0.0, pltpu.roll(own, 1, 1))
        total = total + jnp.where(at_last, 0.0, pltpu.roll(own, cols - 1, 1))
        total = total + image[: plane_rows * per] + image[2 * plane_rows :]
        pieces = []
        for z in range(per):
            for r in range(rows):
                here = lambda q: own[z * plane_rows + q * tiles : z * plane_rows + (q + 1) * tiles]
                if r > 0:
                    low = here(r - 1)
                else:
                    low = jnp.where(tile_index == 0, 0.0, pltpu.roll(here(rows - 1), 1, 0))
                if r < rows - 1:
                    high = here(r + 1)
                else:
                    high = jnp.where(
                        tile_index == tiles - 1, 0.0, pltpu.roll(here(0), tiles - 1, 0)
                    )
                pieces.append(low + high)
        total = total + jnp.concatenate(pieces, axis=0)
        result = 0.125 * (6.0 * own - total)
        result = pltpu.roll(result, lax.rem(h + cols, cols), 1)
        for z in range(per):
            for r in range(rows):
                at = z * plane_rows + r * tiles
                woven[u, pl.ds(r * per + z, tiles, stride=rows * per), :] = result[at : at + tiles]
        out[k] = woven[u].astype(jnp.bfloat16)

    def stored(b):
        span = pl.ds(b * UNROLL, UNROLL)
        return pltpu.make_async_copy(out.at[span], out_hbm.at[span], store_sem.at[b])

    def finish_some(b):
        for u in range(UNROLL):
            finish(u, b * UNROLL + u)
        stored(b).start()

    in_order(NLAG // UNROLL, finish_some)
    in_order(NLAG // UNROLL, lambda b: stored(b).wait())
    wave_store.wait()

    def sent(side):
        for copy in halo_copies(side):
            copy.wait_send()
        wave_copy(side).wait_send()

    each_side(sent)
    for s in range(2):
        in_order(tiles - 1, lambda i: snap_copy(s, lax.rem(me + 1 + i, tiles)).wait_send())


def shards(tiles, now, prev, facies, vel, eps, tilt, src_cell, wavelet, cells, data):
    rows, depth, cols = facies.shape
    per = depth // tiles
    nrec = cells.shape[0]
    block = (per + 2) * 2 * rows
    image_rows = (per + 2) * rows * tiles
    f32 = jnp.float32
    hbm = pl.BlockSpec(memory_space=pltpu.HBM)
    lhs_rows = (rows + 2) * PARTS * STEPS
    filtered, wave = pl.pallas_call(
        functools.partial(kernel, tiles),
        out_shape=(
            jax.ShapeDtypeStruct((NLAG, rows * tiles * per, cols), jnp.bfloat16),
            jax.ShapeDtypeStruct(now.shape, f32),
        ),
        in_specs=[hbm] * 10,
        out_specs=(hbm, hbm),
        scratch_shapes=[
            pltpu.VMEM(prev.shape, f32),
            pltpu.VMEM(facies.shape, jnp.int32),
            pltpu.SMEM(vel.shape, f32),
            pltpu.SMEM(eps.shape, f32),
            pltpu.SMEM(tilt.shape, f32),
            pltpu.SMEM(src_cell.shape, jnp.int32),
            pltpu.SMEM(wavelet.shape, f32),
            pltpu.VMEM((1, nrec), jnp.int32),
            pltpu.VMEM(data.shape, f32),
            pltpu.VMEM((NLAG, rows * tiles * per, cols), jnp.bfloat16),
            pltpu.VMEM(now.shape, f32),
            pltpu.VMEM((2, rows + 2 * HALO, depth, cols), f32),
            pltpu.VMEM((2, rows + 2 * HALO, depth, cols), f32),
            pltpu.VMEM((2, rows + 2, depth, cols), f32),
            pltpu.VMEM((2, rows + 2, depth, cols), f32),
            pltpu.VMEM((2, 2, depth, cols), f32),
            pltpu.VMEM((2, depth, cols), jnp.int32),
            pltpu.VMEM((3, rows + 2, depth, cols), f32),
            pltpu.VMEM((lhs_rows, nrec), f32),
            pltpu.VMEM((lhs_rows, cols), f32),
            pltpu.VMEM((2 * rows * (depth + 2), cols), f32),
            pltpu.VMEM((2, tiles, block, cols), jnp.bfloat16),
            pltpu.VMEM((2, tiles, block, cols), jnp.bfloat16),
            pltpu.VMEM((2, 2, image_rows, cols), f32),
            pltpu.VMEM((NLAG, image_rows, cols), f32),
            pltpu.VMEM((tiles * block, cols), f32),
            pltpu.VMEM((UNROLL, rows * tiles * per, cols), f32),
            pltpu.SemaphoreType.DMA((2, 4)),
            pltpu.SemaphoreType.DMA((2, 4)),
            pltpu.SemaphoreType.DMA((2, tiles)),
            pltpu.SemaphoreType.DMA((2, tiles)),
            pltpu.SemaphoreType.DMA((10,)),
            pltpu.SemaphoreType.DMA((NLAG // UNROLL + 1,)),
            pltpu.SemaphoreType.REGULAR((max(1, tiles.bit_length()),)),
        ],
        compiler_params=pltpu.CompilerParams(collective_id=0, has_side_effects=True),
    )(now, prev, facies, vel, eps, tilt, src_cell, wavelet, cells.reshape(1, nrec), data)
    return filtered.reshape(NLAG, rows * tiles, per, cols), wave


def solution(mesh):
    return jax.shard_map(
        functools.partial(shards, mesh.shape["tile"]),
        mesh=mesh,
        in_specs=(
            P("shot", "tile", None, None),
            P("shot", "tile", None, None),
            P("tile", None, None),
            P(),
            P(),
            P(),
            P("shot"),
            P("shot"),
            P("shot"),
            P(None, "shot"),
        ),
        out_specs=(P("shot", None, "tile", None), P("shot", "tile", None, None)),
        check_vma=False,
    )
```

```python
import functools

import jax
import jax.numpy as jnp
from jax import lax
from jax.experimental import pallas as pl
from jax.experimental.pallas import tpu as pltpu
from jax.sharding import PartitionSpec as P

NLAG = 32
STEPS = 4
HALO = 2
UNROLL = 4
REACH = 4
PARTS = 4


def in_order(count, body):
    def run(i, carry):
        body(i)
        return carry

    lax.fori_loop(0, count, run, 0)


def kernel(
    tiles,
    now,
    prev_in,
    facies_in,
    vel_in,
    eps_in,
    tilt_in,
    src_in,
    wavelet_in,
    cells_in,
    data_in,
    out_hbm,
    wave_hbm,
    prev,
    facies,
    vel_tab,
    eps_tab,
    tilt_tab,
    src_cell,
    wavelet,
    cells,
    data,
    out,
    wave_out,
    ext0,
    ext1,
    mid0,
    mid1,
    prev_halo,
    fac_halo,
    coef,
    lhs,
    surf,
    turned,
    send,
    recv,
    planes,
    part_image,
    staged,
    woven,
    halo_send,
    halo_recv,
    snap_send,
    snap_recv,
    load_sem,
    store_sem,
    near_sem,
):
    rows, depth, cols = facies.shape
    per = depth // tiles
    nrec = data.shape[1]
    ext_rows = rows + 2
    group = 2 * rows
    block = (per + 2) * group
    margin = NLAG // 2
    me = lax.axis_index("tile")
    has_up = me > 0
    has_down = me < tiles - 1

    barrier = pltpu.get_barrier_semaphore()

    def signal_at(semaphore, step):
        for way in (-step, step):
            peer = me + way
            there = (peer >= 0) & (peer < tiles)

            @pl.when(there)
            def _():
                pl.semaphore_signal(semaphore, inc=1, device_id={"tile": peer})

    def wait_at(semaphore, step):
        lower = (me >= step).astype(jnp.int32)
        pl.semaphore_wait(semaphore, lower + (me + step < tiles).astype(jnp.int32))

    near = range(1, min(REACH, tiles - 1) + 1)
    for step in near:
        signal_at(barrier, step)

    reaches = []
    while (REACH << len(reaches)) < tiles - 1:
        reaches.append(REACH << len(reaches))

    loads = [
        pltpu.make_async_copy(src, dst, load_sem.at[n])
        for n, (src, dst) in enumerate(
            (
                (cells_in, cells),
                (data_in, data),
                (facies_in, facies),
                (vel_in, vel_tab),
                (eps_in, eps_tab),
                (tilt_in, tilt_tab),
                (src_in, src_cell),
                (wavelet_in, wavelet),
                (now, ext0.at[:, HALO : HALO + rows]),
                (prev_in, prev),
            )
        )
    ]
    for load in loads:
        load.start()
    zero_plane = jnp.zeros((depth, cols), jnp.float32)
    def clear_side(side, row):
        for f in range(2):
            for i in range(HALO):
                ext0[f, row + i] = zero_plane
                ext1[f, row + i] = zero_plane
            prev_halo[side, f] = zero_plane
        fac_halo[side] = jnp.full((depth, cols), -1, jnp.int32)

    @pl.when(jnp.logical_not(has_up))
    def _():
        clear_side(0, 0)

    @pl.when(jnp.logical_not(has_down))
    def _():
        clear_side(1, rows + HALO)

    reach = min(REACH, tiles - 1)
    pl.semaphore_wait(barrier, jnp.minimum(me, reach) + jnp.minimum(tiles - 1 - me, reach))

    def remote(src, dst, ssem, rsem, peer):
        return pltpu.make_async_remote_copy(
            src_ref=src, dst_ref=dst, send_sem=ssem, recv_sem=rsem, device_id={"tile": peer}
        )

    def halo_copies(side):
        peer = me - 1 if side == 0 else me + 1
        first = 0 if side == 0 else rows - HALO
        edge = 0 if side == 0 else rows - 1
        other = 1 - side
        into = rows + HALO if side == 0 else 0
        sems = lambda n: (halo_send.at[side, n], halo_recv.at[other, n], peer)
        return (
            remote(now.at[:, first : first + HALO], ext0.at[:, into : into + HALO], *sems(0)),
            remote(facies_in.at[edge], fac_halo.at[other], *sems(1)),
            remote(prev_in.at[:, edge], prev_halo.at[other], *sems(2)),
        )

    def wave_copy(side):
        peer = me - 1 if side == 0 else me + 1
        first = HALO if side == 0 else rows
        into = rows + HALO if side == 0 else 0
        return remote(
            ext1.at[:, first : first + HALO], ext1.at[:, into : into + HALO],
            halo_send.at[side, 3], halo_recv.at[1 - side, 3], peer,
        )

    def arrivals(side, count):
        into = 0 if side == 0 else rows + HALO
        peer = me
        sems = lambda n: (halo_send.at[side, n], halo_recv.at[side, n], peer)
        if count == 3:
            return (
                remote(now.at[:, 0:HALO], ext0.at[:, into : into + HALO], *sems(0)),
                remote(facies_in.at[0], fac_halo.at[side], *sems(1)),
                remote(prev_in.at[:, 0], prev_halo.at[side], *sems(2)),
            )
        return (remote(ext1.at[:, HALO : 2 * HALO], ext1.at[:, into : into + HALO], *sems(3)),)

    def each_side(action):
        for side, there in ((0, has_up), (1, has_down)):
            @pl.when(there)
            def _():
                action(side)

    def start_halo(side):
        for copy in halo_copies(side):
            copy.start()

    def wait_halo(side):
        for copy in arrivals(side, 3):
            copy.wait_recv()

    def wait_wave(side):
        for copy in arrivals(side, 1):
            copy.wait_recv()

    if reaches:
        signal_at(near_sem.at[0], reaches[0])
    each_side(start_halo)

    for load in loads[:2]:
        load.wait()

    cell = cells[...]
    column = cell & (cols - 1) if cols & (cols - 1) == 0 else lax.rem(cell, cols)
    onehot = (lax.broadcasted_iota(jnp.int32, (cols, nrec), 0) == column).astype(jnp.float32)
    onehot = onehot.astype(jnp.bfloat16)
    amounts = data[...]
    high = amounts.astype(jnp.bfloat16).astype(jnp.float32)
    rest = amounts - high
    middle = rest.astype(jnp.bfloat16).astype(jnp.float32)
    parts = (high, middle, rest - middle, jnp.zeros_like(high))
    for i in range(ext_rows):
        first = (me * rows + i - 1) * cols
        inside = (cell >= first) & (cell < first + cols)
        for p, part in enumerate(parts):
            at = (i * PARTS + p) * STEPS
            lhs[at : at + STEPS, :] = jnp.where(inside, part, 0.0)
    surf[...] = lax.dot_general(
        lhs[...].astype(jnp.bfloat16), onehot, (((1,), (1,)), ((), ())),
        preferred_element_type=jnp.float32,
    )

    def fill_coef(i, kinds):
        vel = jnp.zeros((depth, cols), jnp.float32)
        eps, tlt = vel, vel
        for n in range(vel_tab.shape[0]):
            here = kinds == n
            vel = jnp.where(here, vel_tab[n], vel)
            eps = jnp.where(here, eps_tab[n], eps)
            tlt = jnp.where(here, tilt_tab[n], tlt)
        coef[0, i] = vel
        coef[1, i] = 1.0 + 2.0 * eps
        coef[2, i] = 0.25 * tlt

    for load in loads[2:]:
        load.wait()
    for i in range(rows):
        fill_coef(i + 1, facies[i])
    turned[0:group, :] = jnp.zeros((group, cols), jnp.float32)
    turned[group * (depth + 1) : group * (depth + 2), :] = jnp.zeros((group, cols), jnp.float32)

    each_side(wait_halo)
    if reaches:
        wait_at(near_sem.at[0], reaches[0])
    if len(reaches) > 1:
        signal_at(near_sem.at[1], reaches[1])
    fill_coef(0, fac_halo[0])
    fill_coef(rows + 1, fac_halo[1])

    lane = lax.broadcasted_iota(jnp.int32, (depth, cols), 1)
    level = lax.broadcasted_iota(jnp.int32, (depth, cols), 0)
    first_lane, last_lane = lane == 0, lane == cols - 1
    first_level, last_level = level == 0, level == depth - 1
    surface_lane = lax.broadcasted_iota(jnp.int32, (1, cols), 1)

    def advance(step, f, i, current, above, below, old):
        right = lambda v: jnp.where(last_lane, 0.0, pltpu.roll(v, cols - 1, 1))
        left = lambda v: jnp.where(first_lane, 0.0, pltpu.roll(v, 1, 1))
        deeper = jnp.where(last_level, 0.0, pltpu.roll(current, depth - 1, 0))
        higher = jnp.where(first_level, 0.0, pltpu.roll(current, 1, 0))
        twice = 2.0 * current
        along_x = right(current) + left(current) - twice
        along_y = above + below - twice
        along_z = deeper + higher - twice
        slope = deeper - higher
        mixed = right(slope) - left(slope)
        operator = coef[1, i] * (along_x + along_y) + along_z + coef[2, i] * mixed
        new = twice - old + coef[0, i] * operator
        if f == 0:
            target = src_cell[0] - (me * rows + i - 1) * cols
            added = jnp.where(surface_lane == target, wavelet[step], 0.0)
        else:
            at = i * PARTS * STEPS + step
            added = surf[at : at + 1, :]
            for p in range(1, 3):
                added = added + surf[at + p * STEPS : at + p * STEPS + 1, :]
        return new + jnp.where(first_level, added, 0.0)

    def outer_step(step, ext, before, into):
        for f in range(2):
            for i in range(ext_rows):
                into[f, i] = advance(
                    step, f, i, ext[f, i + 1], ext[f, i], ext[f, i + 2], before(f, i)
                )

    def inner_step(step, mid, before, store):
        for f in range(2):
            for i in range(rows):
                new = advance(
                    step, f, i + 1, mid[f, i + 1], mid[f, i], mid[f, i + 2], before[f, i + HALO]
                )
                store(f, i, new)
                turned[pl.ds(group + f * rows + i, depth, stride=group), :] = new

    def prev_row(f, i):
        if i == 0:
            return prev_halo[0, f]
        if i == rows + 1:
            return prev_halo[1, f]
        return prev[f, i - 1]

    def pack_snapshot(s):
        for d in range(tiles):
            at = d * per * group
            send[s, d] = turned[at : at + block, :].astype(jnp.bfloat16)

    def snap_copy(s, peer):
        return remote(
            send.at[s, peer], recv.at[s, me], snap_send.at[s, peer], snap_recv.at[s, me], peer
        )

    def send_snapshot(s):
        in_order(tiles - 1, lambda i: snap_copy(s, lax.rem(me + 1 + i, tiles)).start())
        recv[s, me] = send[s, me]

    def await_snapshot(s):
        def body(i):
            peer = lax.rem(me + 1 + i, tiles)
            remote(
                send.at[s, me], recv.at[s, peer], snap_send.at[s, me], snap_recv.at[s, peer], peer
            ).wait_recv()

        in_order(tiles - 1, body)

    def open_snapshot(s):
        staged[...] = recv[s].reshape(tiles * block, cols).astype(jnp.float32)
        for f in range(2):
            for j in range(per + 2):
                for r in range(rows):
                    at = (j * rows + r) * tiles
                    planes[s, f, at : at + tiles, :] = staged[
                        pl.ds(j * group + f * rows + r, tiles, stride=block), :
                    ]

    outer_step(0, ext0, prev_row, mid0)

    def keep_ext1(f, i, new):
        ext1[f, i + HALO] = new

    inner_step(1, mid0, ext0, keep_ext1)
    each_side(lambda side: wave_copy(side).start())
    pack_snapshot(0)
    for n in range(1, len(reaches)):
        wait_at(near_sem.at[n], reaches[n])
        if n + 1 < len(reaches):
            signal_at(near_sem.at[n + 1], reaches[n + 1])
    send_snapshot(0)
    each_side(wait_wave)
    outer_step(2, ext1, lambda f, i: mid0[f, i], mid1)

    def keep_out(f, i, new):
        wave_out[f, i] = new

    inner_step(3, mid1, ext1, keep_out)
    pack_snapshot(1)
    send_snapshot(1)
    wave_store = pltpu.make_async_copy(wave_out, wave_hbm, store_sem.at[NLAG // UNROLL])
    wave_store.start()

    await_snapshot(0)
    open_snapshot(0)

    def pulled(s, k):
        shift = lax.rem(2 * margin - 2 * k + 2 * cols, cols)
        return planes[s, 0] * pltpu.roll(planes[s, 1], shift, 1)

    def first_products(k):
        part_image[k] = pulled(0, k)

    in_order(NLAG, first_products)
    await_snapshot(1)
    open_snapshot(1)

    image_rows = (per + 2) * rows * tiles
    plane_rows = rows * tiles
    image_lane = lax.broadcasted_iota(jnp.int32, (1, cols), 1)
    tile_index = lax.broadcasted_iota(jnp.int32, (tiles, cols), 0)

    def finish(u, k):
        h = k - margin
        far = image_lane + 2 * h
        valid = (far >= 0) & (far < cols)
        image = jnp.where(valid, part_image[k] + pulled(1, k), 0.0)
        image = image.astype(jnp.bfloat16).astype(jnp.float32)
        own = image[plane_rows : plane_rows * (per + 1)]
        at_first = image_lane == lax.rem(cols - h, cols)
        at_last = image_lane == lax.rem(2 * cols - 1 - h, cols)
        total = jnp.where(at_first, 0.0, pltpu.roll(own, 1, 1))
        total = total + jnp.where(at_last, 0.0, pltpu.roll(own, cols - 1, 1))
        total = total + image[: plane_rows * per] + image[2 * plane_rows :]
        pieces = []
        for z in range(per):
            for r in range(rows):
                here = lambda q: own[z * plane_rows + q * tiles : z * plane_rows + (q + 1) * tiles]
                if r > 0:
                    low = here(r - 1)
                else:
                    low = jnp.where(tile_index == 0, 0.0, pltpu.roll(here(rows - 1), 1, 0))
                if r < rows - 1:
                    high = here(r + 1)
                else:
                    high = jnp.where(
                        tile_index == tiles - 1, 0.0, pltpu.roll(here(0), tiles - 1, 0)
                    )
                pieces.append(low + high)
        total = total + jnp.concatenate(pieces, axis=0)
        result = 6.0 * own - total
        result = pltpu.roll(result, lax.rem(h + cols, cols), 1)
        for z in range(per):
            for r in range(rows):
                at = z * plane_rows + r * tiles
                woven[u, pl.ds(r * per + z, tiles, stride=rows * per), :] = result[at : at + tiles]
        out[k] = woven[u].astype(jnp.bfloat16)

    def stored(b):
        span = pl.ds(b * UNROLL, UNROLL)
        return pltpu.make_async_copy(out.at[span], out_hbm.at[span], store_sem.at[b])

    def finish_some(b):
        for u in range(UNROLL):
            finish(u, b * UNROLL + u)
        stored(b).start()

    in_order(NLAG // UNROLL, finish_some)
    in_order(NLAG // UNROLL, lambda b: stored(b).wait())
    wave_store.wait()

    def sent(side):
        for copy in halo_copies(side):
            copy.wait_send()
        wave_copy(side).wait_send()

    each_side(sent)
    for s in range(2):
        in_order(tiles - 1, lambda i: snap_copy(s, lax.rem(me + 1 + i, tiles)).wait_send())


def shards(tiles, now, prev, facies, vel, eps, tilt, src_cell, wavelet, cells, data):
    rows, depth, cols = facies.shape
    per = depth // tiles
    nrec = cells.shape[0]
    block = (per + 2) * 2 * rows
    image_rows = (per + 2) * rows * tiles
    f32 = jnp.float32
    hbm = pl.BlockSpec(memory_space=pltpu.HBM)
    lhs_rows = (rows + 2) * PARTS * STEPS
    filtered, wave = pl.pallas_call(
        functools.partial(kernel, tiles),
        out_shape=(
            jax.ShapeDtypeStruct((NLAG, rows * tiles * per, cols), jnp.bfloat16),
            jax.ShapeDtypeStruct(now.shape, f32),
        ),
        in_specs=[hbm] * 10,
        out_specs=(hbm, hbm),
        scratch_shapes=[
            pltpu.VMEM(prev.shape, f32),
            pltpu.VMEM(facies.shape, jnp.int32),
            pltpu.SMEM(vel.shape, f32),
            pltpu.SMEM(eps.shape, f32),
            pltpu.SMEM(tilt.shape, f32),
            pltpu.SMEM(src_cell.shape, jnp.int32),
            pltpu.SMEM(wavelet.shape, f32),
            pltpu.VMEM((1, nrec), jnp.int32),
            pltpu.VMEM(data.shape, f32),
            pltpu.VMEM((NLAG, rows * tiles * per, cols), jnp.bfloat16),
            pltpu.VMEM(now.shape, f32),
            pltpu.VMEM((2, rows + 2 * HALO, depth, cols), f32),
            pltpu.VMEM((2, rows + 2 * HALO, depth, cols), f32),
            pltpu.VMEM((2, rows + 2, depth, cols), f32),
            pltpu.VMEM((2, rows + 2, depth, cols), f32),
            pltpu.VMEM((2, 2, depth, cols), f32),
            pltpu.VMEM((2, depth, cols), jnp.int32),
            pltpu.VMEM((3, rows + 2, depth, cols), f32),
            pltpu.VMEM((lhs_rows, nrec), f32),
            pltpu.VMEM((lhs_rows, cols), f32),
            pltpu.VMEM((2 * rows * (depth + 2), cols), f32),
            pltpu.VMEM((2, tiles, block, cols), jnp.bfloat16),
            pltpu.VMEM((2, tiles, block, cols), jnp.bfloat16),
            pltpu.VMEM((2, 2, image_rows, cols), f32),
            pltpu.VMEM((NLAG, image_rows, cols), f32),
            pltpu.VMEM((tiles * block, cols), f32),
            pltpu.VMEM((UNROLL, rows * tiles * per, cols), f32),
            pltpu.SemaphoreType.DMA((2, 4)),
            pltpu.SemaphoreType.DMA((2, 4)),
            pltpu.SemaphoreType.DMA((2, tiles)),
            pltpu.SemaphoreType.DMA((2, tiles)),
            pltpu.SemaphoreType.DMA((10,)),
            pltpu.SemaphoreType.DMA((NLAG // UNROLL + 1,)),
            pltpu.SemaphoreType.REGULAR((max(1, tiles.bit_length()),)),
        ],
        compiler_params=pltpu.CompilerParams(collective_id=0, has_side_effects=True),
    )(now, prev, facies, vel, eps, tilt, src_cell, wavelet, cells.reshape(1, nrec), data)
    filtered = filtered * jnp.bfloat16(0.125)
    return filtered.reshape(NLAG, rows * tiles, per, cols), wave


def solution(mesh):
    return jax.shard_map(
        functools.partial(shards, mesh.shape["tile"]),
        mesh=mesh,
        in_specs=(
            P("shot", "tile", None, None),
            P("shot", "tile", None, None),
            P("tile", None, None),
            P(),
            P(),
            P(),
            P("shot"),
            P("shot"),
            P("shot"),
            P(None, "shot"),
        ),
        out_specs=(P("shot", None, "tile", None), P("shot", "tile", None, None)),
        check_vma=False,
    )
```

```python
import functools

import jax
import jax.numpy as jnp
from jax import lax
from jax.experimental import pallas as pl
from jax.experimental.pallas import tpu as pltpu
from jax.sharding import PartitionSpec as P

NLAG = 32
STEPS = 4
HALO = 2
UNROLL = 4
REACH = 4
PARTS = 4


def in_order(count, body):
    def run(i, carry):
        body(i)
        return carry

    lax.fori_loop(0, count, run, 0)


def kernel(
    tiles,
    now,
    prev_in,
    facies_in,
    vel_in,
    eps_in,
    tilt_in,
    src_in,
    wavelet_in,
    cells_in,
    data_in,
    out,
    wave_out,
    prev,
    facies,
    vel_tab,
    eps_tab,
    tilt_tab,
    src_cell,
    wavelet,
    cells,
    data,
    ext0,
    ext1,
    mid0,
    mid1,
    prev_halo,
    fac_halo,
    coef,
    lhs,
    surf,
    turned,
    send,
    recv,
    planes,
    part_image,
    staged,
    woven,
    halo_send,
    halo_recv,
    snap_send,
    snap_recv,
    load_sem,
    near_sem,
):
    rows, depth, cols = facies.shape
    per = depth // tiles
    nrec = data.shape[1]
    ext_rows = rows + 2
    group = 2 * rows
    block = (per + 2) * group
    margin = NLAG // 2
    me = lax.axis_index("tile")
    has_up = me > 0
    has_down = me < tiles - 1

    barrier = pltpu.get_barrier_semaphore()

    def signal_at(semaphore, step):
        for way in (-step, step):
            peer = me + way
            there = (peer >= 0) & (peer < tiles)

            @pl.when(there)
            def _():
                pl.semaphore_signal(semaphore, inc=1, device_id={"tile": peer})

    def wait_at(semaphore, step):
        lower = (me >= step).astype(jnp.int32)
        pl.semaphore_wait(semaphore, lower + (me + step < tiles).astype(jnp.int32))

    near = range(1, min(REACH, tiles - 1) + 1)
    for step in near:
        signal_at(barrier, step)

    reaches = []
    while (REACH << len(reaches)) < tiles - 1:
        reaches.append(REACH << len(reaches))

    loads = [
        pltpu.make_async_copy(src, dst, load_sem.at[n])
        for n, (src, dst) in enumerate(
            (
                (cells_in, cells),
                (data_in, data),
                (facies_in, facies),
                (vel_in, vel_tab),
                (eps_in, eps_tab),
                (tilt_in, tilt_tab),
                (src_in, src_cell),
                (wavelet_in, wavelet),
                (now, ext0.at[:, HALO : HALO + rows]),
                (prev_in, prev),
            )
        )
    ]
    for load in loads:
        load.start()
    zero_plane = jnp.zeros((depth, cols), jnp.float32)
    def clear_side(side, row):
        for f in range(2):
            for i in range(HALO):
                ext0[f, row + i] = zero_plane
                ext1[f, row + i] = zero_plane
            prev_halo[side, f] = zero_plane
        fac_halo[side] = jnp.full((depth, cols), -1, jnp.int32)

    @pl.when(jnp.logical_not(has_up))
    def _():
        clear_side(0, 0)

    @pl.when(jnp.logical_not(has_down))
    def _():
        clear_side(1, rows + HALO)

    reach = min(REACH, tiles - 1)
    pl.semaphore_wait(barrier, jnp.minimum(me, reach) + jnp.minimum(tiles - 1 - me, reach))

    def remote(src, dst, ssem, rsem, peer):
        return pltpu.make_async_remote_copy(
            src_ref=src, dst_ref=dst, send_sem=ssem, recv_sem=rsem, device_id={"tile": peer}
        )

    def halo_copies(side):
        peer = me - 1 if side == 0 else me + 1
        first = 0 if side == 0 else rows - HALO
        edge = 0 if side == 0 else rows - 1
        other = 1 - side
        into = rows + HALO if side == 0 else 0
        sems = lambda n: (halo_send.at[side, n], halo_recv.at[other, n], peer)
        return (
            remote(now.at[:, first : first + HALO], ext0.at[:, into : into + HALO], *sems(0)),
            remote(facies_in.at[edge], fac_halo.at[other], *sems(1)),
            remote(prev_in.at[:, edge], prev_halo.at[other], *sems(2)),
        )

    def wave_copy(side):
        peer = me - 1 if side == 0 else me + 1
        first = HALO if side == 0 else rows
        into = rows + HALO if side == 0 else 0
        return remote(
            ext1.at[:, first : first + HALO], ext1.at[:, into : into + HALO],
            halo_send.at[side, 3], halo_recv.at[1 - side, 3], peer,
        )

    def arrivals(side, count):
        into = 0 if side == 0 else rows + HALO
        peer = me
        sems = lambda n: (halo_send.at[side, n], halo_recv.at[side, n], peer)
        if count == 3:
            return (
                remote(now.at[:, 0:HALO], ext0.at[:, into : into + HALO], *sems(0)),
                remote(facies_in.at[0], fac_halo.at[side], *sems(1)),
                remote(prev_in.at[:, 0], prev_halo.at[side], *sems(2)),
            )
        return (remote(ext1.at[:, HALO : 2 * HALO], ext1.at[:, into : into + HALO], *sems(3)),)

    def each_side(action):
        for side, there in ((0, has_up), (1, has_down)):
            @pl.when(there)
            def _():
                action(side)

    def start_halo(side):
        for copy in halo_copies(side):
            copy.start()

    def wait_halo(side):
        for copy in arrivals(side, 3):
            copy.wait_recv()

    def wait_wave(side):
        for copy in arrivals(side, 1):
            copy.wait_recv()

    if reaches:
        signal_at(near_sem.at[0], reaches[0])
    each_side(start_halo)

    for load in loads[:2]:
        load.wait()

    cell = cells[...]
    column = cell & (cols - 1) if cols & (cols - 1) == 0 else lax.rem(cell, cols)
    onehot = (lax.broadcasted_iota(jnp.int32, (cols, nrec), 0) == column).astype(jnp.float32)
    onehot = onehot.astype(jnp.bfloat16)
    amounts = data[...]
    high = amounts.astype(jnp.bfloat16).astype(jnp.float32)
    rest = amounts - high
    middle = rest.astype(jnp.bfloat16).astype(jnp.float32)
    parts = (high, middle, rest - middle, jnp.zeros_like(high))
    for i in range(ext_rows):
        first = (me * rows + i - 1) * cols
        inside = (cell >= first) & (cell < first + cols)
        for p, part in enumerate(parts):
            at = (i * PARTS + p) * STEPS
            lhs[at : at + STEPS, :] = jnp.where(inside, part, 0.0)
    surf[...] = lax.dot_general(
        lhs[...].astype(jnp.bfloat16), onehot, (((1,), (1,)), ((), ())),
        preferred_element_type=jnp.float32,
    )

    def fill_coef(i, kinds):
        vel = jnp.zeros((depth, cols), jnp.float32)
        eps, tlt = vel, vel
        for n in range(vel_tab.shape[0]):
            here = kinds == n
            vel = jnp.where(here, vel_tab[n], vel)
            eps = jnp.where(here, eps_tab[n], eps)
            tlt = jnp.where(here, tilt_tab[n], tlt)
        coef[0, i] = vel
        coef[1, i] = 1.0 + 2.0 * eps
        coef[2, i] = 0.25 * tlt

    for load in loads[2:]:
        load.wait()
    for i in range(rows):
        fill_coef(i + 1, facies[i])
    turned[0:group, :] = jnp.zeros((group, cols), jnp.float32)
    turned[group * (depth + 1) : group * (depth + 2), :] = jnp.zeros((group, cols), jnp.float32)

    each_side(wait_halo)
    if reaches:
        wait_at(near_sem.at[0], reaches[0])
    if len(reaches) > 1:
        signal_at(near_sem.at[1], reaches[1])
    fill_coef(0, fac_halo[0])
    fill_coef(rows + 1, fac_halo[1])

    lane = lax.broadcasted_iota(jnp.int32, (depth, cols), 1)
    level = lax.broadcasted_iota(jnp.int32, (depth, cols), 0)
    first_lane, last_lane = lane == 0, lane == cols - 1
    first_level, last_level = level == 0, level == depth - 1
    surface_lane = lax.broadcasted_iota(jnp.int32, (1, cols), 1)

    def advance(step, f, i, current, above, below, old):
        right = lambda v: jnp.where(last_lane, 0.0, pltpu.roll(v, cols - 1, 1))
        left = lambda v: jnp.where(first_lane, 0.0, pltpu.roll(v, 1, 1))
        deeper = jnp.where(last_level, 0.0, pltpu.roll(current, depth - 1, 0))
        higher = jnp.where(first_level, 0.0, pltpu.roll(current, 1, 0))
        twice = 2.0 * current
        along_x = right(current) + left(current) - twice
        along_y = above + below - twice
        along_z = deeper + higher - twice
        slope = deeper - higher
        mixed = right(slope) - left(slope)
        operator = coef[1, i] * (along_x + along_y) + along_z + coef[2, i] * mixed
        new = twice - old + coef[0, i] * operator
        if f == 0:
            target = src_cell[0] - (me * rows + i - 1) * cols
            added = jnp.where(surface_lane == target, wavelet[step], 0.0)
        else:
            at = i * PARTS * STEPS + step
            added = surf[at : at + 1, :]
            for p in range(1, 3):
                added = added + surf[at + p * STEPS : at + p * STEPS + 1, :]
        return new + jnp.where(first_level, added, 0.0)

    def outer_step(step, ext, before, into):
        for f in range(2):
            for i in range(ext_rows):
                into[f, i] = advance(
                    step, f, i, ext[f, i + 1], ext[f, i], ext[f, i + 2], before(f, i)
                )

    def inner_step(step, mid, before, store):
        for f in range(2):
            for i in range(rows):
                new = advance(
                    step, f, i + 1, mid[f, i + 1], mid[f, i], mid[f, i + 2], before[f, i + HALO]
                )
                store(f, i, new)
                turned[pl.ds(group + f * rows + i, depth, stride=group), :] = new

    def prev_row(f, i):
        if i == 0:
            return prev_halo[0, f]
        if i == rows + 1:
            return prev_halo[1, f]
        return prev[f, i - 1]

    def pack_snapshot(s):
        for d in range(tiles):
            at = d * per * group
            send[s, d] = turned[at : at + block, :].astype(jnp.bfloat16)

    def snap_copy(s, peer):
        return remote(
            send.at[s, peer], recv.at[s, me], snap_send.at[s, peer], snap_recv.at[s, me], peer
        )

    def send_snapshot(s):
        in_order(tiles - 1, lambda i: snap_copy(s, lax.rem(me + 1 + i, tiles)).start())
        recv[s, me] = send[s, me]

    def await_snapshot(s):
        def body(i):
            peer = lax.rem(me + 1 + i, tiles)
            remote(
                send.at[s, me], recv.at[s, peer], snap_send.at[s, me], snap_recv.at[s, peer], peer
            ).wait_recv()

        in_order(tiles - 1, body)

    def open_snapshot(s):
        staged[...] = recv[s].reshape(tiles * block, cols).astype(jnp.float32)
        for f in range(2):
            for j in range(per + 2):
                for r in range(rows):
                    at = (j * rows + r) * tiles
                    planes[s, f, at : at + tiles, :] = staged[
                        pl.ds(j * group + f * rows + r, tiles, stride=block), :
                    ]

    outer_step(0, ext0, prev_row, mid0)

    def keep_ext1(f, i, new):
        ext1[f, i + HALO] = new

    inner_step(1, mid0, ext0, keep_ext1)
    each_side(lambda side: wave_copy(side).start())
    pack_snapshot(0)
    for n in range(1, len(reaches)):
        wait_at(near_sem.at[n], reaches[n])
        if n + 1 < len(reaches):
            signal_at(near_sem.at[n + 1], reaches[n + 1])
    send_snapshot(0)
    each_side(wait_wave)
    outer_step(2, ext1, lambda f, i: mid0[f, i], mid1)

    def keep_out(f, i, new):
        wave_out[f, i] = new

    inner_step(3, mid1, ext1, keep_out)
    pack_snapshot(1)
    send_snapshot(1)

    await_snapshot(0)
    open_snapshot(0)

    def pulled(s, k):
        shift = lax.rem(2 * margin - 2 * k + 2 * cols, cols)
        return planes[s, 0] * pltpu.roll(planes[s, 1], shift, 1)

    def first_products(k):
        part_image[k] = pulled(0, k)

    in_order(NLAG, first_products)
    await_snapshot(1)
    open_snapshot(1)

    image_rows = (per + 2) * rows * tiles
    plane_rows = rows * tiles
    image_lane = lax.broadcasted_iota(jnp.int32, (1, cols), 1)
    tile_index = lax.broadcasted_iota(jnp.int32, (tiles, cols), 0)

    def finish(u, k):
        h = k - margin
        far = image_lane + 2 * h
        valid = (far >= 0) & (far < cols)
        image = jnp.where(valid, part_image[k] + pulled(1, k), 0.0)
        image = image.astype(jnp.bfloat16).astype(jnp.float32)
        own = image[plane_rows : plane_rows * (per + 1)]
        at_first = image_lane == lax.rem(cols - h, cols)
        at_last = image_lane == lax.rem(2 * cols - 1 - h, cols)
        total = jnp.where(at_first, 0.0, pltpu.roll(own, 1, 1))
        total = total + jnp.where(at_last, 0.0, pltpu.roll(own, cols - 1, 1))
        total = total + image[: plane_rows * per] + image[2 * plane_rows :]
        pieces = []
        for z in range(per):
            for r in range(rows):
                here = lambda q: own[z * plane_rows + q * tiles : z * plane_rows + (q + 1) * tiles]
                if r > 0:
                    low = here(r - 1)
                else:
                    low = jnp.where(tile_index == 0, 0.0, pltpu.roll(here(rows - 1), 1, 0))
                if r < rows - 1:
                    high = here(r + 1)
                else:
                    high = jnp.where(
                        tile_index == tiles - 1, 0.0, pltpu.roll(here(0), tiles - 1, 0)
                    )
                pieces.append(low + high)
        total = total + jnp.concatenate(pieces, axis=0)
        result = 0.125 * (6.0 * own - total)
        result = pltpu.roll(result, lax.rem(h + cols, cols), 1)
        for z in range(per):
            for r in range(rows):
                at = z * plane_rows + r * tiles
                woven[u, pl.ds(r * per + z, tiles, stride=rows * per), :] = result[at : at + tiles]
        out[k] = woven[u].astype(jnp.bfloat16)

    def finish_some(b):
        for u in range(UNROLL):
            finish(u, b * UNROLL + u)

    in_order(NLAG // UNROLL, finish_some)

    def sent(side):
        for copy in halo_copies(side):
            copy.wait_send()
        wave_copy(side).wait_send()

    each_side(sent)
    for s in range(2):
        in_order(tiles - 1, lambda i: snap_copy(s, lax.rem(me + 1 + i, tiles)).wait_send())


def shards(tiles, now, prev, facies, vel, eps, tilt, src_cell, wavelet, cells, data):
    rows, depth, cols = facies.shape
    per = depth // tiles
    nrec = cells.shape[0]
    block = (per + 2) * 2 * rows
    image_rows = (per + 2) * rows * tiles
    f32 = jnp.float32
    vmem = pl.BlockSpec(memory_space=pltpu.VMEM)
    hbm = pl.BlockSpec(memory_space=pltpu.HBM)
    lhs_rows = (rows + 2) * PARTS * STEPS
    filtered, wave = pl.pallas_call(
        functools.partial(kernel, tiles),
        out_shape=(
            pltpu.VMEM((NLAG, rows * tiles * per, cols), jnp.bfloat16),
            pltpu.VMEM(now.shape, f32),
        ),
        in_specs=[hbm] * 10,
        out_specs=(vmem, vmem),
        scratch_shapes=[
            pltpu.VMEM(prev.shape, f32),
            pltpu.VMEM(facies.shape, jnp.int32),
            pltpu.SMEM(vel.shape, f32),
            pltpu.SMEM(eps.shape, f32),
            pltpu.SMEM(tilt.shape, f32),
            pltpu.SMEM(src_cell.shape, jnp.int32),
            pltpu.SMEM(wavelet.shape, f32),
            pltpu.VMEM((1, nrec), jnp.int32),
            pltpu.VMEM(data.shape, f32),
            pltpu.VMEM((2, rows + 2 * HALO, depth, cols), f32),
            pltpu.VMEM((2, rows + 2 * HALO, depth, cols), f32),
            pltpu.VMEM((2, rows + 2, depth, cols), f32),
            pltpu.VMEM((2, rows + 2, depth, cols), f32),
            pltpu.VMEM((2, 2, depth, cols), f32),
            pltpu.VMEM((2, depth, cols), jnp.int32),
            pltpu.VMEM((3, rows + 2, depth, cols), f32),
            pltpu.VMEM((lhs_rows, nrec), f32),
            pltpu.VMEM((lhs_rows, cols), f32),
            pltpu.VMEM((2 * rows * (depth + 2), cols), f32),
            pltpu.VMEM((2, tiles, block, cols), jnp.bfloat16),
            pltpu.VMEM((2, tiles, block, cols), jnp.bfloat16),
            pltpu.VMEM((2, 2, image_rows, cols), f32),
            pltpu.VMEM((NLAG, image_rows, cols), f32),
            pltpu.VMEM((tiles * block, cols), f32),
            pltpu.VMEM((UNROLL, rows * tiles * per, cols), f32),
            pltpu.SemaphoreType.DMA((2, 4)),
            pltpu.SemaphoreType.DMA((2, 4)),
            pltpu.SemaphoreType.DMA((2, tiles)),
            pltpu.SemaphoreType.DMA((2, tiles)),
            pltpu.SemaphoreType.DMA((10,)),
            pltpu.SemaphoreType.REGULAR((max(1, tiles.bit_length()),)),
        ],
        compiler_params=pltpu.CompilerParams(collective_id=0, has_side_effects=True),
    )(now, prev, facies, vel, eps, tilt, src_cell, wavelet, cells.reshape(1, nrec), data)
    return filtered.reshape(NLAG, rows * tiles, per, cols), wave


def solution(mesh):
    return jax.shard_map(
        functools.partial(shards, mesh.shape["tile"]),
        mesh=mesh,
        in_specs=(
            P("shot", "tile", None, None),
            P("shot", "tile", None, None),
            P("tile", None, None),
            P(),
            P(),
            P(),
            P("shot"),
            P("shot"),
            P("shot"),
            P(None, "shot"),
        ),
        out_specs=(P("shot", None, "tile", None), P("shot", "tile", None, None)),
        check_vma=False,
    )
```
